32 devices in a mesh: sym: 4 (over y, x), row: 8 (over z, core).
Axes of the slice: x: 2, y: 2, z: 4, core: 2. Of those that a mesh axis runs over, the one named last changes fastest.
Arguments:
- psi_inner: bfloat16 [4, 6144, 128], P('sym', 'row'), may hold values from -6 to 6
- outer_state: bfloat16 [512, 128, 128], P('sym', 'row'), may hold values from -6 to 6
- hamiltonian: bfloat16 [4, 6144, 6144], P('sym', 'row'), may hold values from -0.078125 to 0.078125
- dipole_up: bfloat16 [4, 6144, 6144], P('sym', 'row'), may hold values from -0.078125 to 0.078125
- dipole_down: bfloat16 [4, 6144, 6144], P('sym', 'row'), may hold values from -0.078125 to 0.078125
- surface_amp: bfloat16 [4, 6144, 512], P('sym', 'row'), may hold values from -0.078125 to 0.078125
- channel_energy: float32 [512], P('sym'), may hold values from 0.2 to 2
- coupling: bfloat16 [512, 128], P('sym'), may hold values from -0.5 to 0.5
- field: float32 [64], replicated, may hold values from 0.5 to 1.5
- channel_sym: int32 [512, 1], replicated, may hold values from 0 to 3; in each aligned block of 128 rows (0 to 127, 128 to 255, ...) at most 48 rows name the same one
Outputs:
- psi_next: bfloat16 [4, 6144, 128], P('sym', 'row')
- outer_next: bfloat16 [512, 128, 128], P('sym', 'row')
The draws below stay inside these ranges and needn't reach their ends.
Inputs may be any that keep to these rules, and one draw needn't show every extreme that they name: `channel_sym`: in each aligned block of 128 channels (one sector) at most 48 channels belong to one symmetry, and exactly 48 do in some sector; every symmetry owns some channel.
All inputs are finite; a program needn't handle non-finite values.
Results may differ from the reference program's by a relative error of at most 0.006.
Values may be sent and summed in bfloat16 or wider, within the bound.
No kernel may reach another device: no remote copies, remote signals or barrier semaphores. Data moves between devices by JAX's collectives and lax.ppermute only.
A program may use at most 128 MiB of HBM per device.

```python
import math
import jax
import jax.numpy as jnp
import numpy as np
from jax import lax

BASIS = 6144
SECTOR_CH = 128
CAPACITY = 48
STATES = 64
SYMMETRIES = 4
CHANNELS = 512
POINTS = 128


def shard_levels(own_key, shape, cuts, smallest, largest):
    def one(dim, blocks):
        draws = jax.random.uniform(jax.random.fold_in(jax.random.fold_in(own_key, 6), dim), (blocks,), jnp.float32, smallest / len(cuts), largest / len(cuts))
        return jnp.repeat(jnp.exp(draws), shape[dim] // blocks).reshape((-1,) + (1,) * (len(shape) - dim - 1))

    level = one(*cuts[0])
    for cut in cuts[1:]:
        level = level * one(*cut)
    return level


def deal_out(own_key, own, number, rows, amount, top, limit, lean):
    ranking = jax.random.permutation(own_key, amount)
    heavy_load, usual = portions_of(amount, rows * top, limit, lean, True), portions_of(amount, rows * top, limit, lean, False)
    places = jnp.arange(amount)

    def named(lengths, turn):
        used = int((lengths > 0).sum())
        fixed = max(1, used // 4)
        shifted = fixed + (places - fixed + turn * (used - fixed)) % max(1, amount - fixed)
        return jnp.zeros((amount,), jnp.int32).at[ranking[jnp.where(places < fixed, places, shifted)]].set(jnp.asarray(lengths, jnp.int32))

    lengths = jnp.where(number % 4 == 0, named(heavy_load, number // 4), named(usual, number - number // 4 - 1))
    mixed = jax.random.permutation(jax.random.fold_in(own, 3), amount)
    donor, taker = mixed[0:amount // 2 * 2:2], mixed[1:amount // 2 * 2:2]
    room = jnp.minimum(lengths[donor] - 1, limit - lengths[taker]) // 2
    room = jnp.where((donor == ranking[0]) | (taker == ranking[0]) | (lengths[taker] == 0), 0, jnp.maximum(room, 0))
    shifted = jax.random.randint(jax.random.fold_in(own, 4), (amount // 2,), 0, 1 << 20) % (room + 1)
    lengths = lengths.at[donor].add(-shifted).at[taker].add(shifted)
    members = jnp.searchsorted(jnp.cumsum(lengths), jnp.arange(rows * top), side="right").astype(jnp.int32)
    listing = members.reshape(top, rows).T
    listing = listing[jax.random.permutation(jax.random.fold_in(own, 1), rows)]
    turn = jax.random.randint(jax.random.fold_in(own, 2), (rows, 1), 0, top)
    return jnp.take_along_axis(listing, (jnp.arange(top)[None, :] + turn) % top, axis=1)


def portions_of(amount, total, limit, slope, full):
    loads = [(1 << 20) // math.isqrt(grade ** slope) + 1 for grade in range(1, amount + 1)]
    largest = limit if full else min(limit, max(-(-total // amount), total * loads[0] // sum(loads)))
    least = 1 if total - largest >= amount - 1 else 0
    given, spare = [largest] + [least] * (amount - 1), total - largest - least * (amount - 1)
    while spare > 0:
        movable = [i for i in range(1, amount) if given[i] < largest] or [i for i in range(1, amount) if given[i] < limit]
        whole, remaining = sum([loads[i] for i in movable]), spare
        for i in movable:
            more = min(limit - given[i], max(1, remaining * loads[i] // whole), spare)
            given[i] = given[i] + more
            spare = spare - more
    return np.array(given)


def bell_draw(key, shape, width, limit, pieces=(), kind=jnp.bfloat16):
    level = shard_levels(key, shape, pieces, -0.22, 0.18) if pieces else 1.0
    entries = jax.random.normal(key, shape, jnp.float32) * width * level
    return jnp.minimum(jnp.maximum(entries, -limit), limit).astype(kind)


def setup_inputs(seed: int = 0) -> dict:
    key_list = jax.random.split(jax.random.key(seed), 11)
    psi_inner = bell_draw(key_list[0], (SYMMETRIES, BASIS, 2 * STATES), 1.0, 6.0, ((0, 4), (1, 8)))
    outer_state = bell_draw(key_list[1], (CHANNELS, POINTS, 2 * STATES), 1.0, 6.0, ((0, 4), (1, 8)))
    hamiltonian = bell_draw(key_list[2], (SYMMETRIES, BASIS, BASIS), BASIS ** -0.5, 0.078125, ((0, 4), (1, 8)))
    dipole_up = bell_draw(key_list[3], (SYMMETRIES, BASIS, BASIS), BASIS ** -0.5, 0.078125, ((0, 4), (1, 8)))
    dipole_down = bell_draw(key_list[4], (SYMMETRIES, BASIS, BASIS), BASIS ** -0.5, 0.078125, ((0, 4), (1, 8)))
    surface_amp = bell_draw(key_list[5], (SYMMETRIES, BASIS, CHANNELS), BASIS ** -0.5, 0.078125, ((0, 4), (1, 8)))
    channel_energy = jnp.clip(jnp.exp(math.log(2.0) - 2.3025851 * jax.random.uniform(key_list[6], (CHANNELS,), jnp.float32) ** shard_levels(key_list[6], (CHANNELS,), ((0, 4),), -0.2, 0.2)), 0.2, 2.0)
    coupling = bell_draw(key_list[7], (CHANNELS, SECTOR_CH), SECTOR_CH ** -0.5, 0.5, ((0, 4),))
    field = jnp.clip(jax.random.uniform(key_list[8], (STATES,), jnp.float32, 0.5, 1.5), 0.5, 1.5)
    channel_sym_keys = jax.random.split(jax.random.fold_in(key_list[9], 1), CHANNELS // SECTOR_CH)
    channel_sym_turns = jax.random.permutation(jax.random.fold_in(key_list[9], 3), CHANNELS // SECTOR_CH)
    channel_sym = jax.vmap(lambda own, number: deal_out(jax.random.fold_in(key_list[9], 2), own, number, SECTOR_CH, SYMMETRIES, 1, CAPACITY, 2))(channel_sym_keys, channel_sym_turns).reshape((CHANNELS, 1))
    return {"psi_inner": psi_inner, "outer_state": outer_state, "hamiltonian": hamiltonian, "dipole_up": dipole_up, "dipole_down": dipole_down, "surface_amp": surface_amp, "channel_energy": channel_energy, "coupling": coupling, "field": field, "channel_sym": channel_sym}


STEP_DT = 0.5
ETA_PEAK = 2.0


def rotate(values, step_scale):
    half_width = values.shape[-1] // 2
    return step_scale * jnp.concatenate([values[..., half_width:], -values[..., :half_width]], axis=-1)


def taylor_term(psi, outer, hamiltonian, dipole_up, dipole_down, surface_amp, channel_energy, coupling, field, channel_sym, step_scale):
    field_cols = jnp.concatenate([field, field])
    sym_numbers = jnp.arange(SYMMETRIES, dtype=jnp.int32)
    member = (channel_sym[:, 0][None, :] == sym_numbers[:, None]).astype(jnp.float32)

    def inner_products(sym_number):
        vector = psi[sym_number]
        return (jnp.dot(hamiltonian[sym_number], vector, preferred_element_type=jnp.float32),
                jnp.dot(dipole_up[sym_number], vector, preferred_element_type=jnp.float32),
                jnp.dot(dipole_down[sym_number], vector, preferred_element_type=jnp.float32),
                jnp.dot(surface_amp[sym_number].T, vector, preferred_element_type=jnp.float32))

    diagonal_part, raised, lowered, projected = lax.map(inner_products, sym_numbers)
    zero_block = jnp.zeros_like(raised[:1])
    from_below = jnp.concatenate([zero_block, raised[:-1]], axis=0)
    from_above = jnp.concatenate([lowered[1:], zero_block], axis=0)
    boundary = jnp.sum(member[:, :, None] * projected, axis=0)
    edge_values = outer[:, 0, :].astype(jnp.float32)
    mismatch = edge_values - boundary
    surf_scale = (BASIS / SECTOR_CH) ** 0.5

    def source_of(sym_number):
        return jnp.dot(surface_amp[sym_number].astype(jnp.float32), member[sym_number][:, None] * mismatch, precision=lax.Precision.HIGHEST)

    sources = lax.map(source_of, sym_numbers)
    inner_h = diagonal_part + field_cols * (from_below + from_above) + surf_scale * sources
    inner_next = rotate(inner_h, step_scale)

    points = jnp.arange(POINTS, dtype=jnp.int32)
    start_abs = (3 * POINTS) // 4
    absorb_ramp = jnp.maximum(points - start_abs, 0).astype(jnp.float32) / (POINTS - start_abs)
    absorb = ETA_PEAK * absorb_ramp * absorb_ramp
    outer_blocks = outer.reshape(SYMMETRIES, SECTOR_CH, POINTS, 2 * STATES)
    coupling_blocks = coupling.reshape(SYMMETRIES, SECTOR_CH, SECTOR_CH)
    energy_blocks = channel_energy.reshape(SYMMETRIES, SECTOR_CH)
    boundary_blocks = boundary.reshape(SYMMETRIES, SECTOR_CH, 2 * STATES)

    def outer_sector(sym_number):
        values = outer_blocks[sym_number].astype(jnp.float32)
        inner_ghost = boundary_blocks[sym_number][:, None, :]
        padded = jnp.concatenate([inner_ghost, values, jnp.zeros_like(inner_ghost)], axis=1)
        laplace = padded[:, 2:] - 2.0 * values + padded[:, :-2]
        channel_mix = jnp.dot(coupling_blocks[sym_number], outer_blocks[sym_number].reshape(SECTOR_CH, POINTS * 2 * STATES), preferred_element_type=jnp.float32).reshape(SECTOR_CH, POINTS, 2 * STATES)
        outer_ham = -0.5 * laplace + energy_blocks[sym_number][:, None, None] * values + field_cols * channel_mix
        return rotate(outer_ham, step_scale) - step_scale * absorb[None, :, None] * values

    outer_next = lax.map(outer_sector, sym_numbers).reshape(CHANNELS, POINTS, 2 * STATES)
    return inner_next, outer_next


def reference(psi_inner, outer_state, hamiltonian, dipole_up, dipole_down, surface_amp, channel_energy, coupling, field, channel_sym):
    first_inner, first_outer = taylor_term(psi_inner, outer_state, hamiltonian, dipole_up, dipole_down, surface_amp, channel_energy, coupling, field, channel_sym, STEP_DT)
    first_inner = first_inner.astype(jnp.bfloat16)
    first_outer = first_outer.astype(jnp.bfloat16)
    second_inner, second_outer = taylor_term(first_inner, first_outer, hamiltonian, dipole_up, dipole_down, surface_amp, channel_energy, coupling, field, channel_sym, 0.5 * STEP_DT)
    psi_next = (psi_inner.astype(jnp.float32) + first_inner.astype(jnp.float32) + second_inner).astype(jnp.bfloat16)
    outer_next = (outer_state.astype(jnp.float32) + first_outer.astype(jnp.float32) + second_outer).astype(jnp.bfloat16)
    return (psi_next, outer_next)
```

```python
import jax
import jax.numpy as jnp
from jax import lax
from jax.experimental import pallas as pl
from jax.experimental.pallas import tpu as pltpu
from jax.sharding import PartitionSpec as P

BASIS = 6144
SECTOR_CH = 128
CAPACITY = 48

STEP_DT = 0.5
ETA_PEAK = 2.0

F32 = jnp.float32
BF16 = jnp.bfloat16


def rotate(values, step_scale):
    half_width = values.shape[-1] // 2
    return step_scale * jnp.concatenate(
        [values[..., half_width:], -values[..., :half_width]], axis=-1
    )


def partner(value, axis, mask):
    count = lax.axis_size(axis)
    return lax.ppermute(value, axis, [(i, i ^ mask) for i in range(count)])


def odd_links(value, axis):
    count = lax.axis_size(axis)
    pairs = []
    for i in range(1, count - 1, 2):
        pairs += [(i, i + 1), (i + 1, i)]
    pairs += [(0, count - 1), (count - 1, 0)]
    return lax.ppermute(value, axis, pairs)


def split(value):
    high = value.astype(BF16)
    return high, (value - high.astype(F32)).astype(BF16)


def partial_kernel(count, first, last, idx_ref, *refs):
    up_refs = refs[:count]
    down_refs = refs[count : 2 * count]
    own_refs = refs[2 * count : 3 * count]
    vec_refs = refs[3 * count : 4 * count]
    rest = refs[4 * count :]
    acc_in = () if first else rest[:3]
    outs = rest[-3:]
    sums = []
    for m, blocks in enumerate((up_refs, down_refs, own_refs)):
        total = None if first else acc_in[m][...]
        for block, vec in zip(blocks, vec_refs):
            term = jnp.dot(block[0], vec[...], preferred_element_type=F32)
            total = term if total is None else total + term
        sums.append(total)
    up, down, own = sums
    if last:
        even = idx_ref[idx_ref.shape[0] - 1] == 0
        outs[0][...] = jnp.where(even, up, down).astype(BF16)
        outs[1][...] = jnp.where(even, down, up).astype(BF16)
    else:
        outs[0][...] = up
        outs[1][...] = down
    outs[2][...] = own


def partial_products(idx, masks, mats, vecs, acc, last, tile=256):
    rows = mats[0].shape[1]
    depth, width = vecs[0].shape
    count = len(masks)
    tile = tile if rows % tile == 0 else rows
    first = acc is None

    def column(mask):
        return pl.BlockSpec((1, tile, depth), lambda i, ref: (0, i, ref[mask]))

    in_specs = [column(mask) for _ in mats for mask in masks]
    in_specs += [pl.BlockSpec((depth, width), lambda i, ref: (0, 0)) for _ in vecs]
    row_spec = pl.BlockSpec((tile, width), lambda i, ref: (i, 0))
    operands = [m for m in mats for _ in masks] + list(vecs)
    if not first:
        in_specs += [row_spec] * 3
        operands += list(acc)
    kinds = (BF16, BF16, F32) if last else (F32, F32, F32)
    size = rows * depth * count * 3
    return pl.pallas_call(
        lambda *refs: partial_kernel(count, first, last, *refs),
        grid_spec=pltpu.PrefetchScalarGridSpec(
            num_scalar_prefetch=1,
            grid=(rows // tile,),
            in_specs=in_specs,
            out_specs=[row_spec] * 3,
        ),
        out_shape=[jax.ShapeDtypeStruct((rows, width), k) for k in kinds],
        compiler_params=pltpu.CompilerParams(vmem_limit_bytes=24 << 20),
        cost_estimate=pl.CostEstimate(
            flops=2 * size * width, bytes_accessed=2 * size, transcendentals=0
        ),
        name="products",
    )(idx, *operands)


def combine_kernel(final, scale, step, flag_ref, *refs):
    own, got_a, got_b, surf, mis_hi, mis_lo, cols = refs[:7]
    extra = refs[7:-1] if final else refs[7:-2]
    use_b = (flag_ref[0] != 0).astype(F32)
    coupled = got_a[...].astype(F32) + use_b * got_b[...].astype(F32)
    source = jnp.dot(surf[...], mis_hi[...], preferred_element_type=F32)
    source += jnp.dot(surf[...], mis_lo[...], preferred_element_type=F32)
    total = own[...] + cols[...] * coupled + scale * source
    width = total.shape[-1]
    lane = lax.broadcasted_iota(jnp.int32, total.shape, 1)
    turned = pltpu.roll(total, width // 2, axis=1)
    term = jnp.where(lane < width // 2, step, -step) * turned
    if final:
        psi, before = extra
        out = psi[...].astype(F32) + before[...].astype(F32) + term
        refs[-1][...] = out.astype(BF16)
    else:
        term = term.astype(BF16)
        refs[-2][...] = term
        refs[-1][...] = lax.dot_general(
            surf[...], term, (((0,), (0,)), ((), ())), preferred_element_type=F32
        )


def combine(flag, own, got_a, got_b, surf, mismatch, cols, step, scale, extra=()):
    rows, width = own.shape
    final = bool(extra)
    hi, lo = split(mismatch)
    operands = [own, got_a, got_b, surf, hi, lo, cols, *extra]
    out_shape = [jax.ShapeDtypeStruct((rows, width), BF16)]
    if not final:
        out_shape.append(jax.ShapeDtypeStruct((surf.shape[1], width), F32))
    vmem = pl.BlockSpec(memory_space=pltpu.VMEM)
    return pl.pallas_call(
        lambda *refs: combine_kernel(final, scale, step, *refs),
        in_specs=[pl.BlockSpec(memory_space=pltpu.SMEM)] + [vmem] * len(operands),
        out_specs=[vmem] * len(out_shape),
        out_shape=out_shape,
        compiler_params=pltpu.CompilerParams(vmem_limit_bytes=16 << 20),
        cost_estimate=pl.CostEstimate(
            flops=6 * rows * width * surf.shape[1],
            bytes_accessed=4 * rows * width * 3,
            transcendentals=0,
        ),
        name="combine",
    )(flag, *operands)


def swapped_step(
    psi_inner,
    outer_state,
    hamiltonian,
    dipole_up,
    dipole_down,
    surface_amp,
    channel_energy,
    coupling,
    field,
    channel_sym,
):
    sym = lax.axis_index("sym").astype(jnp.int32)
    row = lax.axis_index("row").astype(jnp.int32)
    syms = lax.axis_size("sym")
    rows = lax.axis_size("row")
    psi = psi_inner[0]
    width = psi.shape[1]
    sector, points, _ = outer_state.shape
    slots = syms * CAPACITY
    scale = (BASIS / SECTOR_CH) ** 0.5
    field_cols = jnp.concatenate([field, field])
    cols = field_cols[None, :]
    mats = (dipole_up, dipole_down, hamiltonian)
    at_origin = row == 0
    idx = jnp.concatenate([row ^ jnp.arange(rows, dtype=jnp.int32), (sym & 1)[None]])
    flag = ((sym > 0) & (sym < syms - 1)).astype(jnp.int32)[None]

    names = channel_sym[:, 0].reshape(syms, sector)
    lower = (
        lax.broadcasted_iota(jnp.int32, (sector, sector), 0)
        < lax.broadcasted_iota(jnp.int32, (sector, sector), 1)
    )
    held = (names == sym).astype(F32)
    rank = jnp.dot(held, lower.astype(F32), preferred_element_type=F32).astype(jnp.int32)
    block = jnp.arange(syms, dtype=jnp.int32)[:, None] ^ sym
    slot = jnp.where(names == sym, block * CAPACITY + rank, -1).reshape(-1)
    pick = (slot[:, None] == jnp.arange(slots, dtype=jnp.int32)[None, :]).astype(BF16)
    surf = jnp.dot(surface_amp[0], pick, preferred_element_type=F32).astype(BF16)

    mine = lax.dynamic_index_in_dim(names, sym, 0, keepdims=False)
    same = (mine[:, None] == mine[None, :]).astype(F32)
    rank_mine = jnp.sum(same * lower.astype(F32), axis=0).astype(jnp.int32)
    slot_mine = (mine ^ sym) * CAPACITY + rank_mine
    place = (slot_mine[:, None] == jnp.arange(slots, dtype=jnp.int32)[None, :]).astype(BF16)

    def gather_start(vec):
        z2 = partner(vec, "row", 4)
        z1 = partner(vec, "row", 2)
        c0 = partner(vec, "row", 1)
        z3 = partner(z2, "row", 2)
        c1 = partner(z1, "row", 1)
        c2 = partner(z2, "row", 1)
        c3 = partner(z3, "row", 1)
        return {0: vec, 1: c0, 2: z1, 3: c1, 4: z2, 5: c2, 6: z3, 7: c3}

    def products(vecs):
        acc = partial_products(idx, (0, 1), mats, [vecs[0], vecs[1]], None, False)
        acc = partial_products(idx, (2, 3, 4, 5), mats, [vecs[k] for k in (2, 3, 4, 5)], acc, False)
        return partial_products(idx, (6, 7), mats, [vecs[6], vecs[7]], acc, True)

    def row_sum(part):
        for mask in (4, 2, 1):
            part = part + partner(part.astype(BF16), "row", mask).astype(F32)
        return part

    def to_symmetries(stack):
        blocks = stack.reshape(syms, -1, width)
        got = [blocks[0]] + [partner(blocks[k], "sym", k) for k in range(1, syms)]
        return jnp.stack(got)

    vecs = gather_start(psi)

    edge = outer_state[:, 0, :]
    edge32 = edge.astype(F32)
    next32 = outer_state[:, 1, :].astype(F32)
    mix0 = jnp.dot(coupling, edge, preferred_element_type=F32)
    absorb0 = absorb_of(jnp.zeros((), jnp.int32) + row * points, points * rows)
    ham0 = -0.5 * (next32 - 2.0 * edge32) + channel_energy[:, None] * edge32 + cols * mix0
    pre = rotate(ham0, STEP_DT) - STEP_DT * absorb0 * edge32
    pre_hi, pre_lo = split(pre)
    packed = jnp.concatenate([edge, pre_hi, pre_lo], axis=1)
    sorted_edges = lax.dot_general(
        place, packed, (((0,), (0,)), ((), ())), preferred_element_type=F32
    ).astype(BF16)
    sorted_edges = sorted_edges.reshape(syms, CAPACITY, 3, width).transpose(0, 2, 1, 3)
    arrived = to_symmetries(sorted_edges).reshape(syms, 3, CAPACITY, width)
    edge_slots = arrived[:, 0].reshape(slots, width).astype(F32)
    pre_slots = (arrived[:, 1].astype(F32) + arrived[:, 2].astype(F32)).reshape(slots, width)

    part = lax.dot_general(surf, psi, (((0,), (0,)), ((), ())), preferred_element_type=F32)
    mismatch = row_sum(jnp.where(at_origin, edge_slots, 0.0) - part)

    send_a, send_b, own = products(vecs)
    got_a = partner(send_a, "sym", 1)
    got_b = odd_links(send_b, "sym")
    first, part = combine(flag, own, got_a, got_b, surf, mismatch, cols, STEP_DT, scale)

    vecs = gather_start(first)
    boundary = edge_slots - mismatch
    edge_next = (pre_slots + rotate(-0.5 * boundary, STEP_DT)).astype(BF16)
    mismatch2 = row_sum(jnp.where(at_origin, edge_next.astype(F32), 0.0) - part)
    boundary2 = edge_next.astype(F32) - mismatch2
    b_hi, b_lo = split(boundary2)
    back = jnp.stack(
        [v.reshape(syms, CAPACITY, width) for v in (edge_next, b_hi, b_lo)], axis=1
    )
    back = to_symmetries(back).reshape(syms, 3, CAPACITY, width)
    back = back.transpose(0, 2, 1, 3).reshape(slots, 3 * width)
    home = jnp.dot(place, back, preferred_element_type=F32)
    edge_home = home[:, :width]
    boundary_home = home[:, width : 2 * width] + home[:, 2 * width :]

    send_a, send_b, own = products(vecs)
    got_a = partner(send_a, "sym", 1)
    got_b = odd_links(send_b, "sym")
    (psi_next,) = combine(
        flag, own, got_a, got_b, surf, mismatch2, cols, 0.5 * STEP_DT, scale, (psi, first)
    )

    state = outer_state.transpose(1, 0, 2)
    ring = [(i, (i + 1) % rows) for i in range(rows)]
    before = lax.ppermute(state[-2:], "row", ring)
    after = lax.ppermute(state[:2], "row", [(j, i) for i, j in ring])
    before = jnp.where(at_origin, jnp.zeros_like(before), before)
    after = jnp.where(row == rows - 1, jnp.zeros_like(after), after)
    ext = jnp.concatenate([before, state, after], axis=0)
    mix = lax.dot_general(ext, coupling, (((1,), (1,)), ((), ())), preferred_element_type=F32)
    mix = mix.transpose(0, 2, 1)[1:-1]
    energy = channel_energy[None, :, None]
    numbers = row * points + jnp.arange(-1, points + 1, dtype=jnp.int32)
    absorb = absorb_of(numbers, points * rows)[:, None, None]
    wide = ext.astype(F32)
    mid = wide[1:-1]
    ham = -0.5 * (wide[2:] - 2.0 * mid + wide[:-2]) + energy * mid + field_cols * mix
    outer_first = (rotate(ham, STEP_DT) - STEP_DT * absorb * mid).astype(BF16)
    outer_first = jnp.concatenate(
        [
            outer_first[:1],
            jnp.where(at_origin, edge_home.astype(BF16), outer_first[1])[None],
            outer_first[2:-1],
            jnp.where(row == rows - 1, jnp.zeros_like(outer_first[-1:]), outer_first[-1:]),
        ],
        axis=0,
    )
    wide = outer_first.astype(F32)
    wide = jnp.concatenate(
        [jnp.where(at_origin, boundary_home[None], wide[:1]), wide[1:]], axis=0
    )
    mid = wide[1:-1]
    mix = lax.dot_general(
        outer_first[1:-1], coupling, (((1,), (1,)), ((), ())), preferred_element_type=F32
    ).transpose(0, 2, 1)
    ham = -0.5 * (wide[2:] - 2.0 * mid + wide[:-2]) + energy * mid + field_cols * mix
    second = rotate(ham, 0.5 * STEP_DT) - 0.5 * STEP_DT * absorb[1:-1] * mid
    outer_next = (state.astype(F32) + mid + second).astype(BF16).transpose(1, 0, 2)
    return psi_next[None], outer_next


def absorb_of(numbers, total):
    start = 3 * total // 4
    ramp = jnp.maximum(numbers - start, 0).astype(F32) / (total - start)
    return ETA_PEAK * ramp * ramp


def padded_2(value, sides, width):
    for axis, dim in sides:
        devices, length = (lax.axis_size(axis), value.shape[dim])
        up = [(i, (i + 1) % devices) for i in range(devices - 1)]
        down = [(j, i) for i, j in up]
        last = lax.slice_in_dim(value, length - width, length, axis=dim)
        initial = lax.slice_in_dim(value, 0, width, axis=dim)
        before = lax.ppermute(last, axis, up)
        after = lax.ppermute(initial, axis, down)
        value = jnp.concatenate([before, value, after], axis=dim)
    return value


def taylor_term(
    psi_rows,
    outer_block,
    hamiltonian,
    dipole_up,
    dipole_down,
    surface_amp,
    channel_energy,
    coupling,
    field,
    channel_sym,
    step_scale,
):
    sym_index = lax.axis_index("sym")
    row_index = lax.axis_index("row")
    sector_ch = outer_block.shape[0]
    points_dev = outer_block.shape[1]
    width = psi_rows.shape[1]
    field_cols = jnp.concatenate([field, field])
    matrices = (hamiltonian[0], dipole_up[0], dipole_down[0])
    block_rows = lax.all_gather(psi_rows, "row", axis=0, tiled=True)
    diagonal_part, raised, lowered = tuple(
        (jnp.dot(matrix, block_rows, preferred_element_type=jnp.float32) for matrix in matrices)
    )
    stacked = jnp.stack([lowered, raised])
    neighbours = padded_2(stacked, (("sym", 0),), 1)
    coupled = neighbours[0] + neighbours[3]
    amplitudes = surface_amp[0]
    member = (channel_sym[:, 0] == sym_index).astype(jnp.float32)
    partial_proj = member[:, None] * lax.dot_general(
        amplitudes, psi_rows, (((0,), (0,)), ((), ())), preferred_element_type=jnp.float32
    )
    edge_rows = outer_block[:, 0, :]
    placed = jnp.where(row_index == 0, edge_rows.astype(jnp.float32), 0.0)
    edge_full = lax.dynamic_update_slice_in_dim(
        jnp.zeros_like(partial_proj), placed, sym_index * sector_ch, 0
    )
    boundary, edge_values = lax.psum((partial_proj, edge_full), ("sym", "row"))
    mismatch = member[:, None] * (edge_values - boundary)
    boundary_sector = lax.dynamic_slice_in_dim(boundary, sym_index * sector_ch, sector_ch, 0)
    surf_scale = (BASIS / SECTOR_CH) ** 0.5
    source = jnp.dot(amplitudes.astype(jnp.float32), mismatch, precision=lax.Precision.HIGHEST)
    inner_h = diagonal_part + field_cols * coupled + surf_scale * source
    inner_next = rotate(inner_h, step_scale)
    radial_ext = padded_2(outer_block, (("row", 1),), 1)
    values = outer_block.astype(jnp.float32)
    lower_ghost = jnp.where(
        row_index == 0, boundary_sector[:, None, :], radial_ext[:, :1, :].astype(jnp.float32)
    )
    upper_ghost = radial_ext[:, -1:, :].astype(jnp.float32)
    padded = jnp.concatenate([lower_ghost, values, upper_ghost], axis=1)
    laplace = padded[:, 2:] - 2.0 * values + padded[:, :-2]
    channel_mix = jnp.dot(
        coupling,
        outer_block.reshape(sector_ch, points_dev * width),
        preferred_element_type=jnp.float32,
    ).reshape(sector_ch, points_dev, width)
    outer_ham = -0.5 * laplace + channel_energy[:, None, None] * values + field_cols * channel_mix
    total_points = points_dev * lax.axis_size("row")
    points = row_index * points_dev + jnp.arange(points_dev, dtype=jnp.int32)
    start_abs = 3 * total_points // 4
    absorb_ramp = jnp.maximum(points - start_abs, 0).astype(jnp.float32) / (
        total_points - start_abs
    )
    absorb = ETA_PEAK * absorb_ramp * absorb_ramp
    outer_next = rotate(outer_ham, step_scale) - step_scale * absorb[None, :, None] * values
    return (inner_next, outer_next)


def on_device(
    psi_inner,
    outer_state,
    hamiltonian,
    dipole_up,
    dipole_down,
    surface_amp,
    channel_energy,
    coupling,
    field,
    channel_sym,
):
    first_inner, first_outer = taylor_term(
        psi_inner[0],
        outer_state,
        hamiltonian,
        dipole_up,
        dipole_down,
        surface_amp,
        channel_energy,
        coupling,
        field,
        channel_sym,
        STEP_DT,
    )
    first_inner = first_inner.astype(jnp.bfloat16)
    first_outer = first_outer.astype(jnp.bfloat16)
    second_inner, second_outer = taylor_term(
        first_inner,
        first_outer,
        hamiltonian,
        dipole_up,
        dipole_down,
        surface_amp,
        channel_energy,
        coupling,
        field,
        channel_sym,
        0.5 * STEP_DT,
    )
    psi_next = (
        psi_inner[0].astype(jnp.float32) + first_inner.astype(jnp.float32) + second_inner
    ).astype(jnp.bfloat16)
    outer_next = (
        outer_state.astype(jnp.float32) + first_outer.astype(jnp.float32) + second_outer
    ).astype(jnp.bfloat16)
    return (psi_next[None], outer_next)


def solution(mesh):
    quick = mesh.shape["row"] == 8 and mesh.shape["sym"] == 4
    return jax.shard_map(
        swapped_step if quick else on_device,
        mesh=mesh,
        in_specs=(
            P("sym", "row", None),
            P("sym", "row", None),
            P("sym", "row", None),
            P("sym", "row", None),
            P("sym", "row", None),
            P("sym", "row", None),
            P("sym"),
            P("sym", None),
            P(),
            P(),
        ),
        out_specs=(P("sym", "row", None), P("sym", "row", None)),
        check_vma=False,
    )
```
